1024 devices in a mesh: dp: 16 (over y, core), expert: 64 (over z, x).
Axes of the slice: x: 4, y: 8, z: 16, core: 2. Of those that a mesh axis runs over, the one named last changes fastest.
Arguments:
- tokens: bfloat16 [512, 4096], P('expert', 'dp'), may hold values from -6 to 6
- expert_ids: int32 [512, 8], P('expert'), may hold values from 0 to 63, all different within a row; in each aligned block of 8 rows (0 to 7, 8 to 15, ...) at most 3 rows name the same one
- route_weights: float32 [512, 8], P('expert'), may hold values from 0.2 to 1
- w_gate: bfloat16 [64, 4096, 768], P('expert', 'dp'), may hold values from -0.09375 to 0.09375
- w_up: bfloat16 [64, 4096, 768], P('expert', 'dp'), may hold values from -0.09375 to 0.09375
- w_down: bfloat16 [64, 768, 4096], P('expert', None, 'dp'), may hold values from -0.21875 to 0.21875
- grad_out: bfloat16 [512, 4096], P('expert', 'dp'), may hold values from -6 to 6
Outputs:
- layer_out: bfloat16 [512, 4096], P('expert', 'dp')
- input_grad: bfloat16 [512, 4096], P('expert', 'dp')
- gate_weight_grad: bfloat16 [64, 4096, 768], P('expert', 'dp')
- up_weight_grad: bfloat16 [64, 4096, 768], P('expert', 'dp')
- down_weight_grad: bfloat16 [64, 768, 4096], P('expert', None, 'dp')
The draws below stay inside these ranges and needn't reach their ends.
Inputs may be any that keep to these rules, and one draw needn't show every extreme that they name: `expert_ids`: among the 8 tokens of one block no expert is named more than 3 times, and in some block some expert is named exactly 3 times; a token names 8 different experts.
All inputs are finite; a program needn't handle non-finite values.
Results may differ from the reference program's by a relative error of at most 0.028.
Values may be sent and summed in bfloat16 or wider, within the bound.
No kernel may reach another device: no remote copies, remote signals or barrier semaphores. Data moves between devices by JAX's collectives and lax.ppermute only.
A program may use at most 32 MiB of HBM per device.

```python
import math
import jax
import jax.numpy as jnp
import numpy as np
from jax import lax

MODEL_WIDTH = 4096
FF = 768
CHOSEN_EXPERTS = 8
TOKENS_PER_SHARD = 8
EXPERTS = 64
CAP = 3
TOKENS = 512
N_DP = 16
N_EXPERT = 64


def levels(own_key, extent, cuts, low, top_value):
    def one(position, parts):
        draws = jax.random.uniform(jax.random.fold_in(jax.random.fold_in(own_key, 6), position), (parts,), jnp.float32, low / len(cuts), top_value / len(cuts))
        return jnp.repeat(jnp.exp(draws), extent[position] // parts).reshape((-1,) + (1,) * (len(extent) - position - 1))

    factor_of = one(*cuts[0])
    for cut in cuts[1:]:
        factor_of = factor_of * one(*cut)
    return factor_of


def assign_block(stream_key, own, number, rows, count, top, reach, skew):
    order = jax.random.permutation(stream_key, count)
    crowded, usual = load_shares(count, rows * top, reach, skew, True), load_shares(count, rows * top, reach, skew, False)
    places = jnp.arange(count)

    def named(tallies, turn):
        used = int((tallies > 0).sum())
        fixed = max(1, used // 4)
        moved = fixed + (places - fixed + turn * (used - fixed)) % max(1, count - fixed)
        return jnp.zeros((count,), jnp.int32).at[order[jnp.where(places < fixed, places, moved)]].set(jnp.asarray(tallies, jnp.int32))

    tallies = jnp.where(number % 4 == 0, named(crowded, number // 4), named(usual, number - number // 4 - 1))
    mixed = jax.random.permutation(jax.random.fold_in(own, 3), count)
    giver, receiver = mixed[0:count // 2 * 2:2], mixed[1:count // 2 * 2:2]
    slack = jnp.minimum(tallies[giver] - 1, reach - tallies[receiver]) // 2
    slack = jnp.where((giver == order[0]) | (receiver == order[0]) | (tallies[receiver] == 0), 0, jnp.maximum(slack, 0))
    moved = jax.random.randint(jax.random.fold_in(own, 4), (count // 2,), 0, 1 << 20) % (slack + 1)
    tallies = tallies.at[giver].add(-moved).at[receiver].add(moved)
    items = jnp.searchsorted(jnp.cumsum(tallies), jnp.arange(rows * top), side="right").astype(jnp.int32)
    grid = items.reshape(top, rows).T
    grid = grid[jax.random.permutation(jax.random.fold_in(own, 1), rows)]
    turn = jax.random.randint(jax.random.fold_in(own, 2), (rows, 1), 0, top)
    return jnp.take_along_axis(grid, (jnp.arange(top)[None, :] + turn) % top, axis=1)


def load_shares(amount, total, most, lean, full):
    loads = [(1 << 20) // math.isqrt(standing ** lean) + 1 for standing in range(1, amount + 1)]
    largest = most if full else min(most, max(-(-total // amount), total * loads[0] // sum(loads)))
    least = 1 if total - largest >= amount - 1 else 0
    counts, rest = [largest] + [least] * (amount - 1), total - largest - least * (amount - 1)
    while rest > 0:
        movable = [i for i in range(1, amount) if counts[i] < largest] or [i for i in range(1, amount) if counts[i] < most]
        whole, left = sum([loads[i] for i in movable]), rest
        for i in movable:
            addition = min(most - counts[i], max(1, left * loads[i] // whole), rest)
            counts[i] = counts[i] + addition
            rest = rest - addition
    return np.array(counts)


def gaussian(own_key, shape, scale, most, split=(), held_as=jnp.bfloat16):
    entries = scale * jax.random.normal(own_key, shape, jnp.float32)
    if split:
        entries = entries * levels(own_key, shape, split, -0.22, 0.18)
    return jnp.clip(entries, -most, most).astype(held_as)


def setup_inputs(seed: int = 0) -> dict:
    arg_keys = jax.random.split(jax.random.key(seed), 8)
    tokens = gaussian(arg_keys[0], (TOKENS, MODEL_WIDTH), 1.0, 6.0, ((0, 64), (1, 16)))
    expert_ids_keys = jax.random.split(jax.random.fold_in(arg_keys[1], 1), TOKENS // TOKENS_PER_SHARD)
    expert_ids_turns = jax.random.permutation(jax.random.fold_in(arg_keys[1], 3), TOKENS // TOKENS_PER_SHARD)
    expert_ids = jax.vmap(lambda own, number: assign_block(jax.random.fold_in(arg_keys[1], 2), own, number, TOKENS_PER_SHARD, EXPERTS, CHOSEN_EXPERTS, CAP, 1))(expert_ids_keys, expert_ids_turns).reshape((TOKENS, CHOSEN_EXPERTS))
    route_weights = jnp.clip(0.2 + 0.8 * jax.random.uniform(arg_keys[2], (TOKENS, CHOSEN_EXPERTS), jnp.float32) ** levels(arg_keys[2], (TOKENS, CHOSEN_EXPERTS), ((0, 64),), -0.2, 0.2), 0.2, 1.0)
    w_gate = gaussian(arg_keys[3], (EXPERTS, MODEL_WIDTH, FF), MODEL_WIDTH ** -0.5, 0.09375, ((0, 64), (1, 16)))
    w_up = gaussian(arg_keys[4], (EXPERTS, MODEL_WIDTH, FF), MODEL_WIDTH ** -0.5, 0.09375, ((0, 64), (1, 16)))
    w_down = gaussian(arg_keys[5], (EXPERTS, FF, MODEL_WIDTH), FF ** -0.5, 0.21875, ((0, 64), (2, 16)))
    grad_out = gaussian(arg_keys[6], (TOKENS, MODEL_WIDTH), 1.0, 6.0, ((0, 64), (1, 16)))
    return dict(tokens=tokens, expert_ids=expert_ids, route_weights=route_weights, w_gate=w_gate, w_up=w_up, w_down=w_down, grad_out=grad_out)


def slot_table(id_block, experts, capacity):
    flat_ids = id_block.reshape(-1).astype(jnp.int32)
    onehot = (flat_ids[:, None] == jnp.arange(experts, dtype=jnp.int32)[None, :]).astype(jnp.int32)
    before = jnp.cumsum(onehot, axis=0) - onehot
    slot_index = jnp.sum(before * onehot, axis=1)
    target = flat_ids * capacity + slot_index
    row_index = jnp.arange(experts * capacity, dtype=jnp.int32)
    return (row_index[:, None] == target[None, :]).astype(jnp.bfloat16)


def block_sum(form, left, right):
    products = jnp.einsum(form, left, right)
    rounded = lax.optimization_barrier(products.astype(jnp.bfloat16))
    return jnp.sum(rounded.astype(jnp.float32), axis=0)


def gate_grads(hidden_grad, gate, up_value):
    sigmoid_gate = jax.nn.sigmoid(gate)
    silu_gate = gate * sigmoid_gate
    gate_grad = (hidden_grad * up_value * sigmoid_gate * (1.0 + gate * (1.0 - sigmoid_gate))).astype(jnp.bfloat16)
    up_grad = (hidden_grad * silu_gate).astype(jnp.bfloat16)
    return gate_grad, up_grad


def expert_pass(packed):
    expert_in, expert_grad, gate_matrix, up_matrix, down_matrix = packed
    slices = MODEL_WIDTH // N_DP
    row_count = expert_in.shape[0]
    in_blocks = expert_in.astype(jnp.float32).reshape(row_count, N_DP, slices)
    gate = block_sum("rbd,bdf->brf", in_blocks, gate_matrix.astype(jnp.float32).reshape(N_DP, slices, FF))
    up_value = block_sum("rbd,bdf->brf", in_blocks, up_matrix.astype(jnp.float32).reshape(N_DP, slices, FF))
    hidden = (gate * jax.nn.sigmoid(gate) * up_value).astype(jnp.bfloat16)
    expert_out = jnp.dot(hidden, down_matrix, preferred_element_type=jnp.float32).astype(jnp.bfloat16)
    grad_blocks = expert_grad.astype(jnp.float32).reshape(row_count, N_DP, slices)
    hidden_grad = block_sum("rbd,fbd->brf", grad_blocks, down_matrix.astype(jnp.float32).reshape(FF, N_DP, slices))
    gate_grad, up_grad = gate_grads(hidden_grad, gate, up_value)
    down_grad = jnp.dot(hidden.T, expert_grad, preferred_element_type=jnp.float32).astype(jnp.bfloat16)
    gate_weight = jnp.dot(expert_in.T, gate_grad, preferred_element_type=jnp.float32).astype(jnp.bfloat16)
    up_weight = jnp.dot(expert_in.T, up_grad, preferred_element_type=jnp.float32).astype(jnp.bfloat16)
    input_rows = (jnp.dot(gate_grad, gate_matrix.T, preferred_element_type=jnp.float32)
                  + jnp.dot(up_grad, up_matrix.T, preferred_element_type=jnp.float32)).astype(jnp.bfloat16)
    return expert_out, input_rows, gate_weight, up_weight, down_grad


def to_sources(rows):
    return rows.reshape(EXPERTS, N_EXPERT, CAP, MODEL_WIDTH).transpose(1, 0, 2, 3).reshape(N_EXPERT, EXPERTS * CAP, MODEL_WIDTH)


def reference(tokens, expert_ids, route_weights, w_gate, w_up, w_down, grad_out):
    id_blocks = expert_ids.reshape(N_EXPERT, TOKENS_PER_SHARD, CHOSEN_EXPERTS)
    tables = jax.vmap(lambda id_block: slot_table(id_block, EXPERTS, CAP))(id_blocks)
    slot_table_float = tables.astype(jnp.float32)
    weight_rep = route_weights.reshape(N_EXPERT, TOKENS_PER_SHARD * CHOSEN_EXPERTS)
    token_replicas = jnp.repeat(tokens.reshape(N_EXPERT, TOKENS_PER_SHARD, MODEL_WIDTH), CHOSEN_EXPERTS, axis=1).astype(jnp.float32)
    gradient_rounding = (jnp.repeat(grad_out.reshape(N_EXPERT, TOKENS_PER_SHARD, MODEL_WIDTH), CHOSEN_EXPERTS, axis=1).astype(jnp.float32)
                  * weight_rep[:, :, None]).astype(jnp.bfloat16)
    gradient_rounding = lax.optimization_barrier(gradient_rounding)
    dispatch_token_rows = jnp.einsum("euc,ecg->eug", slot_table_float, token_replicas).astype(jnp.bfloat16)
    dispatch_gradients = jnp.einsum("euc,ecg->eug", slot_table_float, gradient_rounding.astype(jnp.float32)).astype(jnp.bfloat16)
    expert_in = dispatch_token_rows.reshape(N_EXPERT, EXPERTS, CAP, MODEL_WIDTH).transpose(1, 0, 2, 3).reshape(EXPERTS, N_EXPERT * CAP, MODEL_WIDTH)
    expert_grad = dispatch_gradients.reshape(N_EXPERT, EXPERTS, CAP, MODEL_WIDTH).transpose(1, 0, 2, 3).reshape(EXPERTS, N_EXPERT * CAP, MODEL_WIDTH)
    results = lax.map(expert_pass, (expert_in, expert_grad, w_gate, w_up, w_down))
    output_row_block = to_sources(results[0]).astype(jnp.float32)
    gradient_row_block = to_sources(results[1]).astype(jnp.float32)
    backward_output = jnp.einsum("pat,paz->ptz", slot_table_float, output_row_block).reshape(N_EXPERT, TOKENS_PER_SHARD, CHOSEN_EXPERTS, MODEL_WIDTH)
    backward_input = jnp.einsum("pat,paz->ptz", slot_table_float, gradient_row_block).reshape(N_EXPERT, TOKENS_PER_SHARD, CHOSEN_EXPERTS, MODEL_WIDTH)
    weights_full = route_weights.reshape(N_EXPERT, TOKENS_PER_SHARD, CHOSEN_EXPERTS)
    layer_out = jnp.sum(backward_output * weights_full[:, :, :, None], axis=2).astype(jnp.bfloat16).reshape(TOKENS, MODEL_WIDTH)
    input_grad = jnp.sum(backward_input, axis=2).astype(jnp.bfloat16).reshape(TOKENS, MODEL_WIDTH)
    return layer_out, input_grad, results[2], results[3], results[4]
```

```python
import jax
import jax.numpy as jnp
from jax import lax
from jax.sharding import PartitionSpec as P

BF = jnp.bfloat16
F32 = jnp.float32


def slot_table(id_block, experts, capacity):
    flat_ids = id_block.reshape(-1)
    onehot = (flat_ids[:, None] == jnp.arange(experts, dtype=jnp.int32)[None, :]).astype(jnp.int32)
    before = jnp.cumsum(onehot, axis=0) - onehot
    slot_index = jnp.sum(before * onehot, axis=1)
    target = flat_ids * capacity + slot_index
    row_index = jnp.arange(experts * capacity, dtype=jnp.int32)
    return (row_index[:, None] == target[None, :]).astype(BF)


def gate_grads(hidden_grad, gate, up_value):
    sigmoid_gate = jax.nn.sigmoid(gate)
    silu_gate = gate * sigmoid_gate
    gate_grad = (
        hidden_grad * up_value * sigmoid_gate * (1.0 + gate * (1.0 - sigmoid_gate))
    ).astype(BF)
    up_grad = (hidden_grad * silu_gate).astype(BF)
    return (gate_grad, up_grad)


def mm(left, right, lc, rc):
    return lax.dot_general(left, right, (((lc,), (rc,)), ((), ())), preferred_element_type=F32)


def local(tokens, expert_ids, route_weights, w_gate, w_up, w_down, grad_out):
    tok_rows, slices = tokens.shape
    top_count = expert_ids.shape[1]
    experts = lax.axis_size("expert")
    dp = lax.axis_size("dp")
    capacity = min(tok_rows, 3 * tok_rows * top_count // experts)
    rows = experts * capacity
    gate_matrix, up_matrix, down_matrix = w_gate[0], w_up[0], w_down[0]
    ff = gate_matrix.shape[1]
    half = ff // 2
    chips = dp // 2
    group = rows // chips
    lanes = 2 * slices // 128

    table = slot_table(expert_ids, experts, capacity)
    weight_flat = route_weights.reshape(-1)
    token_rep = jnp.repeat(tokens, top_count, axis=0)
    grad_rep = (
        jnp.repeat(grad_out, top_count, axis=0).astype(F32) * weight_flat[:, None]
    ).astype(BF)
    packed = mm(table, jnp.concatenate([token_rep, grad_rep], axis=1), 1, 0).astype(BF)
    received = lax.all_to_all(
        packed.reshape(experts, capacity, lanes, 128), "expert", split_axis=0, concat_axis=0, tiled=True
    ).reshape(rows, 2 * slices)
    expert_in, expert_grad = received[:, :slices], received[:, slices:]

    gate_part = mm(expert_in, gate_matrix, 1, 0).astype(BF)
    up_part = mm(expert_in, up_matrix, 1, 0).astype(BF)
    grad_part = mm(expert_grad, down_matrix, 1, 1).astype(BF)

    def halves(c):
        cut = slice(c * half, (c + 1) * half)
        return jnp.concatenate([gate_part[:, cut], up_part[:, cut], grad_part[:, cut]], axis=1)

    stacked = jnp.stack([halves(0).reshape(chips, group, 3 * half), halves(1).reshape(chips, group, 3 * half)], axis=1)
    parts = lax.all_to_all(
        stacked.reshape(dp, group, 3 * half), "dp", split_axis=0, concat_axis=0, tiled=True
    )
    sums = jnp.sum(parts.astype(F32), axis=0)
    gate, up, hidden_grad = sums[:, :half], sums[:, half : 2 * half], sums[:, 2 * half :]
    hidden_piece = (gate * jax.nn.sigmoid(gate) * up).astype(BF)
    gate_grad_piece, up_grad_piece = gate_grads(hidden_grad, gate, up)
    pieces = jnp.concatenate([hidden_piece, gate_grad_piece, up_grad_piece], axis=1)

    gathered = lax.all_gather(pieces, "dp", axis=0, tiled=True).reshape(chips, 2, group, 3 * half)
    cols = [gathered[:, c].reshape(rows, 3 * half) for c in range(2)]
    hidden, gate_grad, up_grad = (
        jnp.concatenate([cols[c][:, i * half : (i + 1) * half] for c in range(2)], axis=1) for i in range(3)
    )

    expert_out = mm(hidden, down_matrix, 1, 0).astype(BF)
    input_rows = (mm(gate_grad, gate_matrix, 1, 1) + mm(up_grad, up_matrix, 1, 1)).astype(BF)
    back = lax.all_to_all(
        jnp.concatenate([expert_out, input_rows], axis=1).reshape(experts, capacity, lanes, 128),
        "expert", split_axis=0, concat_axis=0, tiled=True,
    ).reshape(rows, 2 * slices)

    down_grad = mm(hidden, expert_grad, 0, 0).astype(BF)
    gate_weight = mm(expert_in, gate_grad, 0, 0).astype(BF)
    up_weight = mm(expert_in, up_grad, 0, 0).astype(BF)

    choice = mm(table, back, 0, 0).reshape(tok_rows, top_count, 2 * slices)
    layer_out = jnp.sum(choice[:, :, :slices] * route_weights[:, :, None], axis=1).astype(BF)
    input_grad = jnp.sum(choice[:, :, slices:], axis=1).astype(BF)
    return (layer_out, input_grad, gate_weight[None], up_weight[None], down_grad[None])


def solution(mesh):
    return jax.shard_map(
        local,
        mesh=mesh,
        in_specs=(
            P("expert", "dp"),
            P("expert", None),
            P("expert", None),
            P("expert", "dp", None),
            P("expert", "dp", None),
            P("expert", None, "dp"),
            P("expert", "dp"),
        ),
        out_specs=(
            P("expert", "dp"),
            P("expert", "dp"),
            P("expert", "dp", None),
            P("expert", "dp", None),
            P("expert", None, "dp"),
        ),
        check_vma=False,
    )
```

```python
import jax
import jax.numpy as jnp
from jax import lax
from jax.experimental import pallas as pl
from jax.experimental.pallas import tpu as pltpu
from jax.sharding import PartitionSpec as P

BF = jnp.bfloat16
F32 = jnp.float32
VMEM = pl.BlockSpec(memory_space=pltpu.VMEM)


def dot(left, right, lc, rc, precision=None):
    return lax.dot_general(
        left, right, (((lc,), (rc,)), ((), ())), preferred_element_type=F32, precision=precision
    )


def dispatch_body(capacity, ids_ref, weights_ref, tokens_ref, grads_ref, rows_ref, pick_ref, scaled_ref):
    tok, top = ids_ref.shape
    rows = rows_ref.shape[0]
    experts = rows // capacity
    width = tokens_ref.shape[1]
    ids, weights = ids_ref[...], weights_ref[...]
    expert = lax.broadcasted_iota(jnp.int32, (tok, experts), 1)
    named = jnp.zeros((tok, experts), F32)
    weight = jnp.zeros((tok, experts), F32)
    for k in range(top):
        hit = ids[:, k : k + 1] == expert
        named = named + jnp.where(hit, 1.0, 0.0)
        weight = weight + jnp.where(hit, weights[:, k : k + 1], 0.0)
    earlier = lax.broadcasted_iota(jnp.int32, (tok, tok), 0) > lax.broadcasted_iota(jnp.int32, (tok, tok), 1)
    slot = dot(jnp.where(earlier, 1.0, 0.0), named, 1, 0)
    row = lax.broadcasted_iota(jnp.int32, (rows, experts), 0)
    owner = lax.broadcasted_iota(jnp.int32, (rows, experts), 1)
    first = owner * capacity
    spread = jnp.where((row >= first) & (row < first + capacity), 1.0, 0.0)
    row_id = lax.broadcasted_iota(jnp.int32, (rows, tok), 0)
    row_slot = lax.rem(row_id, capacity).astype(F32)
    chosen = dot(spread, jnp.where(named > 0.5, slot, -1.0), 1, 1)
    pick = jnp.where(jnp.abs(chosen - row_slot) < 0.5, 1.0, 0.0)
    row_weight = dot(spread, weight, 1, 1, lax.Precision.HIGHEST)
    scale = jnp.sum(pick * row_weight, axis=1, keepdims=True)
    rows_ref[:, :width] = dot(pick, tokens_ref[...].astype(F32), 1, 0).astype(BF)
    rows_ref[:, width:] = (dot(pick, grads_ref[...].astype(F32), 1, 0) * scale).astype(BF)
    pick_ref[...] = pick
    scaled_ref[...] = pick * scale


def dispatch(ids, weights, tokens, grads, rows, capacity):
    tok, width = tokens.shape

    def body(*refs):
        dispatch_body(capacity, *refs)

    return pl.pallas_call(
        body,
        out_shape=(
            pltpu.VMEM((rows, 2 * width), BF),
            pltpu.VMEM((rows, tok), F32),
            pltpu.VMEM((rows, tok), F32),
        ),
        in_specs=[VMEM] * 4,
        out_specs=(VMEM,) * 3,
    )(ids, weights, tokens, grads)


def near(*arrays):
    return [pltpu.with_memory_space_constraint(x, pltpu.VMEM) for x in arrays]


def share(side, rows_ref, gate_ref, up_ref, down_ref):
    width = rows_ref.shape[1] // 2
    half = gate_ref.shape[2] // 2
    cut = pl.ds(pl.multiple_of(side * half, half), half)
    yield slice(0, half), dot(rows_ref[:, :width], gate_ref[0, :, cut], 1, 0)
    yield slice(half, 2 * half), dot(rows_ref[:, :width], up_ref[0, :, cut], 1, 0)
    yield slice(2 * half, 3 * half), dot(rows_ref[:, width:], down_ref[0, cut, :], 1, 1)


def theirs_body(rows_ref, gate_ref, up_ref, down_ref, theirs_ref):
    core = lax.rem(lax.axis_index("dp"), 2)
    for cols, value in share(1 - core, rows_ref, gate_ref, up_ref, down_ref):
        theirs_ref[:, cols] = value.astype(BF)


def theirs_share(received, matrices):
    return pl.pallas_call(
        theirs_body,
        out_shape=pltpu.VMEM((received.shape[0], 3 * matrices[0].shape[2] // 2), BF),
        in_specs=[VMEM] * 4,
        out_specs=VMEM,
    )(*near(received), *matrices)


def pair_body(both_ref, rows_ref, gate_ref, up_ref, down_ref, pair_ref):
    rows = rows_ref.shape[0]
    core = lax.rem(lax.axis_index("dp"), 2)
    other = pl.ds(pl.multiple_of((1 - core) * rows, rows), rows)
    for cols, value in share(core, rows_ref, gate_ref, up_ref, down_ref):
        pair_ref[:, cols] = (value + both_ref[other, cols].astype(F32)).astype(BF)


def pair_share(both, received, matrices):
    return pl.pallas_call(
        pair_body,
        out_shape=pltpu.VMEM((received.shape[0], both.shape[1]), BF),
        in_specs=[VMEM] * 5,
        out_specs=VMEM,
    )(*near(both, received), *matrices)


def finish_body(
    back_ref, pick_ref, scaled_ref, rows_ref, low_ref, high_ref, out_ref, in_ref, gate_ref, up_ref, down_ref,
    out_buf, in_buf, gate_buf, up_buf, down_buf, sems,
):
    width = rows_ref.shape[1] // 2
    half = low_ref.shape[1] // 3
    sides = (low_ref, high_ref)
    expert_in, expert_grad = rows_ref[:, :width], rows_ref[:, width:]
    stores = [
        pltpu.make_async_copy(buf, out, sems.at[i])
        for i, (buf, out) in enumerate(
            (
                (gate_buf, gate_ref.at[0]),
                (up_buf, up_ref.at[0]),
                (down_buf, down_ref.at[0]),
                (out_buf, out_ref),
                (in_buf, in_ref),
            )
        )
    ]
    for i, buf in enumerate((gate_buf, up_buf)):
        for c, side in enumerate(sides):
            grad = side[:, (i + 1) * half : (i + 2) * half]
            buf[:, c * half : (c + 1) * half] = dot(expert_in, grad, 0, 0).astype(BF)
        stores[i].start()
    for c, side in enumerate(sides):
        down_buf[c * half : (c + 1) * half, :] = dot(side[:, :half], expert_grad, 0, 0).astype(BF)
    stores[2].start()
    out_buf[...] = dot(scaled_ref[...], back_ref[:, :width].astype(F32), 0, 0, lax.Precision.HIGHEST).astype(BF)
    stores[3].start()
    in_buf[...] = dot(pick_ref[...], back_ref[:, width:].astype(F32), 0, 0).astype(BF)
    stores[4].start()
    for store in stores:
        store.wait()


def finish(back, pick, scaled, received, low, high):
    width, half = received.shape[1] // 2, low.shape[1] // 3
    tok = pick.shape[1]
    shapes = ((tok, width), (tok, width), (1, width, 2 * half), (1, width, 2 * half), (1, 2 * half, width))
    return pl.pallas_call(
        finish_body,
        out_shape=tuple(jax.ShapeDtypeStruct(s, BF) for s in shapes),
        in_specs=[VMEM] * 6,
        out_specs=(pl.BlockSpec(memory_space=pl.ANY),) * 5,
        scratch_shapes=[pltpu.VMEM(s[-2:], BF) for s in shapes] + [pltpu.SemaphoreType.DMA((5,))],
    )(*near(back, pick, scaled, received, low, high))


def back_body(low_ref, high_ref, gate_ref, up_ref, down_ref, rows_ref):
    width = rows_ref.shape[1] // 2
    half = low_ref.shape[1] // 3
    out, back = None, None
    for c, side in enumerate((low_ref, high_ref)):
        cut = slice(c * half, (c + 1) * half)
        one = dot(side[:, :half], down_ref[0, cut, :], 1, 0)
        two = dot(side[:, half : 2 * half], gate_ref[0, :, cut], 1, 1)
        two = two + dot(side[:, 2 * half :], up_ref[0, :, cut], 1, 1)
        out, back = (one, two) if c == 0 else (out + one, back + two)
    rows_ref[:, :width] = out.astype(BF)
    rows_ref[:, width:] = back.astype(BF)


def back_rows(low, high, matrices):
    return pl.pallas_call(
        back_body,
        out_shape=pltpu.VMEM((low.shape[0], 2 * matrices[0].shape[1]), BF),
        in_specs=[VMEM] * 5,
        out_specs=VMEM,
    )(*near(low, high), *matrices)


def gate_grads(hidden_grad, gate, up_value):
    sigmoid_gate = jax.nn.sigmoid(gate)
    silu_gate = gate * sigmoid_gate
    gate_grad = (
        hidden_grad * up_value * sigmoid_gate * (1.0 + gate * (1.0 - sigmoid_gate))
    ).astype(BF)
    up_grad = (hidden_grad * silu_gate).astype(BF)
    return (gate_grad, up_grad)


def local(tokens, expert_ids, route_weights, w_gate, w_up, w_down, grad_out):
    tok_rows, slices = tokens.shape
    top_count = expert_ids.shape[1]
    experts = lax.axis_size("expert")
    dp = lax.axis_size("dp")
    capacity = min(tok_rows, 3 * tok_rows * top_count // experts)
    rows = experts * capacity
    half = w_gate.shape[2] // 2
    chips = dp // 2
    group = rows // chips
    lanes = 2 * slices // 128

    packed, pick, scaled = dispatch(expert_ids, route_weights, tokens, grad_out, rows, capacity)
    matrices = near(w_gate, w_up, w_down)
    received = lax.all_to_all(
        packed.reshape(experts, capacity, lanes, 128), "expert", split_axis=0, concat_axis=0, tiled=True
    ).reshape(rows, 2 * slices)

    theirs = theirs_share(received, matrices)
    both = lax.all_gather(
        theirs, "dp", axis=0, tiled=True, axis_index_groups=[[2 * i, 2 * i + 1] for i in range(chips)]
    )
    pair = pair_share(both, received, matrices)
    same_core = [[c + 2 * i for i in range(chips)] for c in range(2)]
    parts = lax.all_to_all(
        pair.reshape(chips, group, 3 * half), "dp", split_axis=0, concat_axis=0, tiled=True,
        axis_index_groups=same_core,
    )
    sums = jnp.sum(parts.astype(F32), axis=0)
    gate, up, hidden_grad = sums[:, :half], sums[:, half : 2 * half], sums[:, 2 * half :]
    hidden_piece = (gate * jax.nn.sigmoid(gate) * up).astype(BF)
    gate_grad_piece, up_grad_piece = gate_grads(hidden_grad, gate, up)
    pieces = jnp.concatenate([hidden_piece, gate_grad_piece, up_grad_piece], axis=1)

    gathered = lax.all_gather(pieces, "dp", axis=0, tiled=True).reshape(chips, 2, group, 3 * half)
    low, high = (gathered[:, c].reshape(rows, 3 * half) for c in range(2))

    packed_back = back_rows(low, high, matrices)
    back = lax.all_to_all(
        packed_back.reshape(experts, capacity, lanes, 128), "expert", split_axis=0, concat_axis=0, tiled=True
    ).reshape(rows, 2 * slices)
    return finish(back, pick, scaled, received, low, high)


def solution(mesh):
    return jax.shard_map(
        local,
        mesh=mesh,
        in_specs=(
            P("expert", "dp"),
            P("expert", None),
            P("expert", None),
            P("expert", "dp", None),
            P("expert", "dp", None),
            P("expert", None, "dp"),
            P("expert", "dp"),
        ),
        out_specs=(
            P("expert", "dp"),
            P("expert", "dp"),
            P("expert", "dp", None),
            P("expert", "dp", None),
            P("expert", None, "dp"),
        ),
        check_vma=False,
    )
```

```python
import jax
import jax.numpy as jnp
from jax import lax
from jax.experimental import pallas as pl
from jax.experimental.pallas import tpu as pltpu
from jax.sharding import PartitionSpec as P

BF = jnp.bfloat16
F32 = jnp.float32
VMEM = pl.BlockSpec(memory_space=pltpu.VMEM)


def dot(left, right, lc, rc, precision=None):
    return lax.dot_general(
        left, right, (((lc,), (rc,)), ((), ())), preferred_element_type=F32, precision=precision
    )


def dispatch_body(capacity, ids_ref, weights_ref, tokens_ref, grads_ref, rows_ref, pick_ref, scaled_ref):
    tok, top = ids_ref.shape
    rows = rows_ref.shape[0]
    experts = rows // capacity
    width = tokens_ref.shape[1]
    ids, weights = ids_ref[...], weights_ref[...]
    expert = lax.broadcasted_iota(jnp.int32, (tok, experts), 1)
    named = jnp.zeros((tok, experts), F32)
    weight = jnp.zeros((tok, experts), F32)
    for k in range(top):
        hit = ids[:, k : k + 1] == expert
        named = named + jnp.where(hit, 1.0, 0.0)
        weight = weight + jnp.where(hit, weights[:, k : k + 1], 0.0)
    earlier = lax.broadcasted_iota(jnp.int32, (tok, tok), 0) > lax.broadcasted_iota(jnp.int32, (tok, tok), 1)
    slot = dot(jnp.where(earlier, 1.0, 0.0), named, 1, 0)
    row = lax.broadcasted_iota(jnp.int32, (rows, experts), 0)
    owner = lax.broadcasted_iota(jnp.int32, (rows, experts), 1)
    first = owner * capacity
    spread = jnp.where((row >= first) & (row < first + capacity), 1.0, 0.0)
    row_id = lax.broadcasted_iota(jnp.int32, (rows, tok), 0)
    row_slot = lax.rem(row_id, capacity).astype(F32)
    chosen = dot(spread, jnp.where(named > 0.5, slot, -1.0), 1, 1)
    pick = jnp.where(jnp.abs(chosen - row_slot) < 0.5, 1.0, 0.0)
    row_weight = dot(spread, weight, 1, 1, lax.Precision.HIGHEST)
    scale = jnp.sum(pick * row_weight, axis=1, keepdims=True)
    rows_ref[:, :width] = dot(pick, tokens_ref[...].astype(F32), 1, 0).astype(BF)
    rows_ref[:, width:] = (dot(pick, grads_ref[...].astype(F32), 1, 0) * scale).astype(BF)
    pick_ref[...] = pick
    scaled_ref[...] = pick * scale


def dispatch(ids, weights, tokens, grads, rows, capacity):
    tok, width = tokens.shape

    def body(*refs):
        dispatch_body(capacity, *refs)

    return pl.pallas_call(
        body,
        out_shape=(
            pltpu.VMEM((rows, 2 * width), BF),
            pltpu.VMEM((rows, tok), F32),
            pltpu.VMEM((rows, tok), F32),
        ),
        in_specs=[VMEM] * 4,
        out_specs=(VMEM,) * 3,
    )(ids, weights, tokens, grads)


def near(*arrays):
    return [pltpu.with_memory_space_constraint(x, pltpu.VMEM) for x in arrays]


def share(side, rows_ref, gate_ref, up_ref, down_ref):
    width = rows_ref.shape[1] // 2
    half = gate_ref.shape[2] // 2
    cut = pl.ds(pl.multiple_of(side * half, half), half)
    yield slice(0, half), dot(rows_ref[:, :width], gate_ref[0, :, cut], 1, 0)
    yield slice(half, 2 * half), dot(rows_ref[:, :width], up_ref[0, :, cut], 1, 0)
    yield slice(2 * half, 3 * half), dot(rows_ref[:, width:], down_ref[0, cut, :], 1, 1)


def theirs_body(rows_ref, gate_ref, up_ref, down_ref, theirs_ref):
    core = lax.rem(lax.axis_index("dp"), 2)
    for cols, value in share(1 - core, rows_ref, gate_ref, up_ref, down_ref):
        theirs_ref[:, cols] = value.astype(BF)


def theirs_share(received, matrices):
    return pl.pallas_call(
        theirs_body,
        out_shape=pltpu.VMEM((received.shape[0], 3 * matrices[0].shape[2] // 2), BF),
        in_specs=[VMEM] * 4,
        out_specs=VMEM,
    )(*near(received), *matrices)


def pair_body(both_ref, rows_ref, gate_ref, up_ref, down_ref, pair_ref):
    rows = rows_ref.shape[0]
    core = lax.rem(lax.axis_index("dp"), 2)
    other = pl.ds(pl.multiple_of((1 - core) * rows, rows), rows)
    for cols, value in share(core, rows_ref, gate_ref, up_ref, down_ref):
        pair_ref[:, cols] = (value + both_ref[other, cols].astype(F32)).astype(BF)


def pair_share(both, received, matrices):
    return pl.pallas_call(
        pair_body,
        out_shape=pltpu.VMEM((received.shape[0], both.shape[1]), BF),
        in_specs=[VMEM] * 5,
        out_specs=VMEM,
    )(*near(both, received), *matrices)


def weight_grads_body(rows_ref, low_ref, high_ref, gate_ref, up_ref, down_ref, gate_buf, up_buf, down_buf, sems):
    width = rows_ref.shape[1] // 2
    half = low_ref.shape[1] // 3
    sides = (low_ref, high_ref)
    expert_in, expert_grad = rows_ref[:, :width], rows_ref[:, width:]
    stores = [
        pltpu.make_async_copy(buf, out.at[0], sems.at[i])
        for i, (buf, out) in enumerate(((gate_buf, gate_ref), (up_buf, up_ref), (down_buf, down_ref)))
    ]
    for i, buf in enumerate((gate_buf, up_buf)):
        for c, side in enumerate(sides):
            grad = side[:, (i + 1) * half : (i + 2) * half]
            buf[:, c * half : (c + 1) * half] = dot(expert_in, grad, 0, 0).astype(BF)
        stores[i].start()
    for c, side in enumerate(sides):
        down_buf[c * half : (c + 1) * half, :] = dot(side[:, :half], expert_grad, 0, 0).astype(BF)
    stores[2].start()
    for store in stores:
        store.wait()


def weight_grads(received, low, high):
    width, half = received.shape[1] // 2, low.shape[1] // 3
    shapes = ((1, width, 2 * half), (1, width, 2 * half), (1, 2 * half, width))
    return pl.pallas_call(
        weight_grads_body,
        out_shape=tuple(jax.ShapeDtypeStruct(s, BF) for s in shapes),
        in_specs=[VMEM] * 3,
        out_specs=(pl.BlockSpec(memory_space=pl.ANY),) * 3,
        scratch_shapes=[pltpu.VMEM(s[-2:], BF) for s in shapes] + [pltpu.SemaphoreType.DMA((3,))],
    )(*near(received, low, high))


def combine_body(back_ref, pick_ref, scaled_ref, out_ref, in_ref):
    width = out_ref.shape[1]
    out_ref[...] = dot(scaled_ref[...], back_ref[:, :width].astype(F32), 0, 0, lax.Precision.HIGHEST).astype(BF)
    in_ref[...] = dot(pick_ref[...], back_ref[:, width:].astype(F32), 0, 0).astype(BF)


def combine(back, pick, scaled):
    shape = jax.ShapeDtypeStruct((pick.shape[1], back.shape[1] // 2), BF)
    return pl.pallas_call(
        combine_body, out_shape=(shape, shape), in_specs=[VMEM] * 3, out_specs=(VMEM, VMEM)
    )(*near(back, pick, scaled))


def back_body(low_ref, high_ref, gate_ref, up_ref, down_ref, rows_ref):
    width = rows_ref.shape[1] // 2
    half = low_ref.shape[1] // 3
    out, back = None, None
    for c, side in enumerate((low_ref, high_ref)):
        cut = slice(c * half, (c + 1) * half)
        one = dot(side[:, :half], down_ref[0, cut, :], 1, 0)
        two = dot(side[:, half : 2 * half], gate_ref[0, :, cut], 1, 1)
        two = two + dot(side[:, 2 * half :], up_ref[0, :, cut], 1, 1)
        out, back = (one, two) if c == 0 else (out + one, back + two)
    rows_ref[:, :width] = out.astype(BF)
    rows_ref[:, width:] = back.astype(BF)


def back_rows(low, high, matrices):
    return pl.pallas_call(
        back_body,
        out_shape=pltpu.VMEM((low.shape[0], 2 * matrices[0].shape[1]), BF),
        in_specs=[VMEM] * 5,
        out_specs=VMEM,
    )(*near(low, high), *matrices)


def gate_grads(hidden_grad, gate, up_value):
    sigmoid_gate = jax.nn.sigmoid(gate)
    silu_gate = gate * sigmoid_gate
    gate_grad = (
        hidden_grad * up_value * sigmoid_gate * (1.0 + gate * (1.0 - sigmoid_gate))
    ).astype(BF)
    up_grad = (hidden_grad * silu_gate).astype(BF)
    return (gate_grad, up_grad)


def local(tokens, expert_ids, route_weights, w_gate, w_up, w_down, grad_out):
    tok_rows, slices = tokens.shape
    top_count = expert_ids.shape[1]
    experts = lax.axis_size("expert")
    dp = lax.axis_size("dp")
    capacity = min(tok_rows, 3 * tok_rows * top_count // experts)
    rows = experts * capacity
    half = w_gate.shape[2] // 2
    chips = dp // 2
    group = rows // chips
    lanes = 2 * slices // 128

    packed, pick, scaled = dispatch(expert_ids, route_weights, tokens, grad_out, rows, capacity)
    matrices = near(w_gate, w_up, w_down)
    received = lax.all_to_all(
        packed.reshape(experts, capacity, lanes, 128), "expert", split_axis=0, concat_axis=0, tiled=True
    ).reshape(rows, 2 * slices)

    theirs = theirs_share(received, matrices)
    both = lax.all_gather(
        theirs, "dp", axis=0, tiled=True, axis_index_groups=[[2 * i, 2 * i + 1] for i in range(chips)]
    )
    pair = pair_share(both, received, matrices)
    same_core = [[c + 2 * i for i in range(chips)] for c in range(2)]
    parts = lax.all_to_all(
        pair.reshape(chips, group, 3 * half), "dp", split_axis=0, concat_axis=0, tiled=True,
        axis_index_groups=same_core,
    )
    sums = jnp.sum(parts.astype(F32), axis=0)
    gate, up, hidden_grad = sums[:, :half], sums[:, half : 2 * half], sums[:, 2 * half :]
    hidden_piece = (gate * jax.nn.sigmoid(gate) * up).astype(BF)
    gate_grad_piece, up_grad_piece = gate_grads(hidden_grad, gate, up)
    pieces = jnp.concatenate([hidden_piece, gate_grad_piece, up_grad_piece], axis=1)

    gathered = lax.all_gather(pieces, "dp", axis=0, tiled=True).reshape(chips, 2, group, 3 * half)
    low, high = (gathered[:, c].reshape(rows, 3 * half) for c in range(2))

    packed_back = back_rows(low, high, matrices)
    back = lax.all_to_all(
        packed_back.reshape(experts, capacity, lanes, 128), "expert", split_axis=0, concat_axis=0, tiled=True
    ).reshape(rows, 2 * slices)
    grads = weight_grads(received, low, high)
    return (*combine(back, pick, scaled), *grads)


def solution(mesh):
    return jax.shard_map(
        local,
        mesh=mesh,
        in_specs=(
            P("expert", "dp"),
            P("expert", None),
            P("expert", None),
            P("expert", "dp", None),
            P("expert", "dp", None),
            P("expert", None, "dp"),
            P("expert", "dp"),
        ),
        out_specs=(
            P("expert", "dp"),
            P("expert", "dp"),
            P("expert", "dp", None),
            P("expert", "dp", None),
            P("expert", None, "dp"),
        ),
        check_vma=False,
    )
```
